256 devices in a mesh: pipe: 2 (over core), ctx: 32 (over y, z), tp: 4 (over x).
Axes of the slice: x: 4, y: 4, z: 8, core: 2. Of those that a mesh axis runs over, the one named last changes fastest.
Arguments:
- mamba_input: bfloat16 [2, 2048, 8192], P(None, 'ctx', 'tp')
- gate_input: bfloat16 [2, 2048, 8192], P(None, 'ctx', 'tp'), may hold values from -6 to 6
- bc_input: bfloat16 [2, 2048, 2, 2048], P(None, 'ctx', None, 'tp'), may hold values from -0.8984375 to 0.8984375
- step_raw: float32 [2, 2048, 64], P(None, 'ctx', 'tp'), may hold values from -4 to 4
- decay_log: float32 [64], P('tp')
- skip_gain: float32 [64], P('tp'), may hold values from 0.5 to 1.5
- conv_input: float32 [4, 8192], P(None, 'tp'), may hold values from -3 to 3
- conv_bc: float32 [4, 2, 2048], P(None, None, 'tp'), may hold values from -3 to 3
- norm_gain: float32 [8192], P('tp'), may hold values from 0.5 to 1.5
- keys_values: bfloat16 [2, 2048, 2, 1024], P(None, 'ctx', None, 'tp')
Outputs:
- attended: bfloat16 [2, 2048, 8192], P('pipe', 'ctx', 'tp')
The draws below stay inside these ranges and needn't reach their ends.
All inputs are finite; a program needn't handle non-finite values.
Results may differ from the reference program's by a relative error of at most 0.006.
Values may be sent and summed in bfloat16 or wider, within the bound.
A program may use at most 320 MiB of HBM per device.

```python
import math
import jax
import jax.numpy as jnp
from jax import lax

HEADS = 64
HEAD_DIM = 128
STATE = 256
GROUPS = 8
KV_HEADS = 8
CONV = 4
TOK_DEV = 64
MICRO = 2
SEQ = 2048


def draw_mamba_input(key, part):
    shape = (MICRO, SEQ, HEADS * HEAD_DIM)
    values = jax.random.truncated_normal(jax.random.fold_in(key, 612), -6.0, 6.0, shape, jnp.float32)
    return values.astype(jnp.bfloat16)


def draw_decay_log(key, part):
    first_key = jax.random.fold_in(key, 101)
    second_key = jax.random.fold_in(key, 202)
    third_key = jax.random.fold_in(key, 303)
    fast_share = 0.3
    chance = jax.random.uniform(first_key, (HEADS,), jnp.float32)
    fast_rate = jnp.exp(jax.random.uniform(second_key, (HEADS,), jnp.float32, math.log(1.0 / 40.0), math.log(1.0 / 20.0)))
    spread_rate = jnp.exp(jax.random.uniform(third_key, (HEADS,), jnp.float32, math.log(0.1 / SEQ), math.log(1.0 / (2.0 * TOK_DEV))))
    return jnp.log(jnp.where(chance < fast_share, fast_rate, spread_rate)).astype(jnp.float32)


def draw_keys_values(key, part):
    base = jax.random.truncated_normal(jax.random.fold_in(key, 404), -4.0, 4.0, (MICRO, SEQ, 2, KV_HEADS * HEAD_DIM), jnp.float32)
    return base.astype(jnp.bfloat16)


def block_scale(rng, dims, cuts, least, top_value):
    gain = 1.0
    for dim, parts in cuts:
        draws = jax.random.uniform(jax.random.fold_in(jax.random.fold_in(rng, 6), dim), (parts,), jnp.float32, least / len(cuts), top_value / len(cuts))
        gain = gain * jnp.repeat(jnp.exp(draws), dims[dim] // parts).reshape((-1,) + (1,) * (len(dims) - 1 - dim))
    return gain


def centred(rng, shape, scale, bound, pieces=(), kind=jnp.bfloat16):
    values = jax.random.normal(rng, shape, jnp.float32) * scale
    if len(pieces) > 0:
        values = block_scale(rng, shape, pieces, -0.22, 0.18) * values
    return jnp.clip(values, min=-bound, max=bound).astype(kind)


def setup_inputs(seed: int = 0) -> dict:
    key_list = jax.random.split(jax.random.key(seed), 11)
    mamba_input = draw_mamba_input(jax.random.fold_in(key_list[10], 71), 0)
    gate_input = centred(key_list[1], (MICRO, SEQ, HEADS * HEAD_DIM), 1.0, 6.0, ((1, 32), (2, 4)))
    bc_input = centred(key_list[2], (MICRO, SEQ, 2, GROUPS * STATE), 0.15, 0.8984375, ((1, 32), (3, 4)))
    step_raw = centred(key_list[3], (MICRO, SEQ, HEADS), 1.0, 4.0, ((1, 32), (2, 4)), jnp.float32)
    decay_log = draw_decay_log(jax.random.fold_in(key_list[10], 71), 0)
    skip_gain = jnp.clip(0.5 + 1.0 * jax.random.uniform(key_list[5], (HEADS,), jnp.float32) ** block_scale(key_list[5], (HEADS,), ((0, 4),), -0.2, 0.2), 0.5, 1.5)
    conv_input = centred(key_list[6], (CONV, HEADS * HEAD_DIM), CONV ** -0.5, 3.0, ((1, 4),), jnp.float32)
    conv_bc = centred(key_list[7], (CONV, 2, GROUPS * STATE), CONV ** -0.5, 3.0, ((2, 4),), jnp.float32)
    norm_gain = jnp.clip(1.0 + 0.1 * jax.random.normal(key_list[8], (HEADS * HEAD_DIM,), jnp.float32), 0.5, 1.5)
    keys_values = draw_keys_values(jax.random.fold_in(key_list[10], 71), 0)
    return dict(mamba_input=mamba_input, gate_input=gate_input, bc_input=bc_input, step_raw=step_raw, decay_log=decay_log, skip_gain=skip_gain, conv_input=conv_input, conv_bc=conv_bc, norm_gain=norm_gain, keys_values=keys_values)


def causal_conv(values_in, weight):
    taps = weight.shape[0]
    length = values_in.shape[0]
    lead_zeros = jnp.zeros((taps - 1,) + values_in.shape[1:], values_in.dtype)
    padded = jnp.concatenate([lead_zeros, values_in], axis=0).astype(jnp.float32)
    running = weight[0] * padded[0:length]
    for offset in range(1, taps):
        running = running + weight[offset] * padded[offset:offset + length]
    return jax.nn.silu(running).astype(jnp.bfloat16)

def mamba_layer(inputs, gates, inbc, raw_steps, decay_log, skip_gain, conv_input, conv_bc, norm_gain):
    conv_out = causal_conv(inputs, conv_input)
    bc_out = causal_conv(inbc, conv_bc)
    per_group = HEADS // GROUPS
    block_count = SEQ // TOK_DEV
    signal = conv_out.reshape(block_count, TOK_DEV, GROUPS, per_group, HEAD_DIM)
    b_part = bc_out[:, 0].reshape(block_count, TOK_DEV, GROUPS, STATE)
    c_part = bc_out[:, 1].reshape(block_count, TOK_DEV, GROUPS, STATE)
    steps_dt = jax.nn.softplus(raw_steps).reshape(block_count, TOK_DEV, GROUPS, per_group)
    decay_rate = -jnp.exp(decay_log).reshape(GROUPS, per_group)
    skip_view = skip_gain.reshape(GROUPS, per_group)[None, :, :, None]

    def one_block(carried_state, item):
        block_signal, block_b, block_c, block_dt = item
        cumul = jnp.cumsum(block_dt * decay_rate, axis=0)
        order = jnp.arange(TOK_DEV, dtype=jnp.int32)
        lower_mask = (order[:, None] >= order[None, :])[:, :, None, None]
        gap_matrix = jnp.where(lower_mask, cumul[:, None] - cumul[None, :], -1e+30)
        decay_mat = jnp.exp(gap_matrix)
        scores_cb = jnp.einsum('tgn,sgn->gts', block_c.astype(jnp.float32), block_b.astype(jnp.float32))
        weights = scores_cb[:, None] * jnp.transpose(decay_mat, (2, 3, 0, 1)) * jnp.transpose(block_dt, (1, 2, 0))[:, :, None, :]
        weights = lax.optimization_barrier(weights.astype(jnp.bfloat16)).astype(jnp.float32)
        inner_part = jnp.einsum('gkts,sgkp->tgkp', weights, block_signal.astype(jnp.float32))
        carried = jnp.exp(cumul)[..., None] * jnp.einsum('tgn,gkpn->tgkp', block_c.astype(jnp.float32), carried_state, precision=lax.Precision.HIGHEST)
        mixed_out = inner_part + carried + skip_view * block_signal.astype(jnp.float32)
        tail_decay = jnp.exp(cumul[-1][None] - cumul) * block_dt
        weighted = block_signal.astype(jnp.float32) * tail_decay[..., None]
        weighted = lax.optimization_barrier(weighted.astype(jnp.bfloat16)).astype(jnp.float32)
        local_state = jnp.einsum('sgkp,sgn->gkpn', weighted, block_b.astype(jnp.float32))
        next_state = jnp.exp(cumul[-1])[..., None, None] * carried_state + local_state
        return (next_state, mixed_out)
    start_state = jnp.zeros((GROUPS, per_group, HEAD_DIM, STATE), jnp.float32)
    _, mixed_all = lax.scan(one_block, start_state, (signal, b_part, c_part, steps_dt))
    gated = mixed_all.reshape(SEQ, HEADS * HEAD_DIM) * jax.nn.silu(gates.astype(jnp.float32))
    mean_square = lax.optimization_barrier(jnp.mean(gated * gated, axis=1))
    return (gated * lax.rsqrt(mean_square + 1e-05)[:, None] * norm_gain).astype(jnp.bfloat16)

def attention(queries, stacked_kv):
    per_kv = HEADS // KV_HEADS
    factor = 1.0 / math.sqrt(HEAD_DIM)
    query_view = queries.reshape(SEQ // TOK_DEV, TOK_DEV, KV_HEADS, per_kv, HEAD_DIM)
    keys = stacked_kv[:, 0].reshape(SEQ, KV_HEADS, HEAD_DIM).astype(jnp.float32)
    values = stacked_kv[:, 1].reshape(SEQ, KV_HEADS, HEAD_DIM).astype(jnp.float32)
    key_pos = jnp.arange(SEQ, dtype=jnp.int32)

    def one_block(item):
        block_index, query_block = item
        logits = jnp.einsum('tgkp,sgp->gkts', query_block.astype(jnp.float32), keys) * factor
        query_pos = block_index * TOK_DEV + jnp.arange(TOK_DEV, dtype=jnp.int32)
        valid = key_pos[None, :] <= query_pos[:, None]
        masked = jnp.where(valid, logits, -1e+30)
        row_max = lax.optimization_barrier(jnp.max(masked, axis=-1))
        probs = jnp.where(valid, jnp.exp(logits - row_max[..., None]), 0.0)
        totals = lax.optimization_barrier(jnp.sum(probs, axis=-1))
        rounded = lax.optimization_barrier(probs.astype(jnp.bfloat16)).astype(jnp.float32)
        output = jnp.einsum('gkts,sgp->tgkp', rounded, values) / jnp.transpose(totals, (2, 0, 1))[..., None]
        return output.reshape(TOK_DEV, HEADS * HEAD_DIM).astype(jnp.bfloat16)
    blocks = lax.map(one_block, (jnp.arange(SEQ // TOK_DEV, dtype=jnp.int32), query_view))
    return blocks.reshape(SEQ, HEADS * HEAD_DIM)

def reference(mamba_input, gate_input, bc_input, step_raw, decay_log, skip_gain, conv_input, conv_bc, norm_gain, keys_values):
    results = []
    for micro_index in range(MICRO):
        queries = mamba_layer(mamba_input[micro_index], gate_input[micro_index], bc_input[micro_index], step_raw[micro_index], decay_log, skip_gain, conv_input, conv_bc, norm_gain)
        results.append(attention(queries, keys_values[micro_index]))
    return jnp.stack(results)
```

```python
import math

import jax
import jax.numpy as jnp
from jax import lax
from jax.sharding import PartitionSpec as P

STATE = 256


def passed_along(value, axis, steps):
    count = lax.axis_size(axis)
    first, last = (max(0, -steps), min(count, count - steps))
    return lax.ppermute(value, axis, [(source, source + steps) for source in range(first, last)])


def local(
    mamba_input,
    gate_input,
    bc_input,
    step_raw,
    decay_log,
    skip_gain,
    conv_input,
    conv_bc,
    norm_gain,
    keys_values,
):
    row_count = mamba_input.shape[1]
    feature_width = mamba_input.shape[2]
    heads_here = step_raw.shape[2]
    groups_here = bc_input.shape[3] // STATE
    head_dim = feature_width // heads_here
    kv_here = keys_values.shape[3] // head_dim
    per_group = heads_here // groups_here
    per_kv = heads_here // kv_here
    taps = conv_input.shape[0]
    rim_rows = taps - 1
    position = lax.axis_index("ctx") * row_count
    factor = 1.0 / math.sqrt(head_dim)

    def causal_conv(current, previous, weight):
        joined = jnp.concatenate([previous, current], axis=0).astype(jnp.float32)
        running = weight[0] * joined[0:row_count]
        for offset in range(1, taps):
            running = running + weight[offset] * joined[offset : offset + row_count]
        return jax.nn.silu(running).astype(jnp.bfloat16)

    def pick(array, micro_index):
        return lax.dynamic_slice_in_dim(array, micro_index, 1, 0)[0]

    def mamba_layer(micro_index):
        inputs = pick(mamba_input, micro_index)
        gates = pick(gate_input, micro_index)
        inbc = pick(bc_input, micro_index)
        raw_steps = pick(step_raw, micro_index)
        tail_input, tail_bc = passed_along(
            (inputs[row_count - rim_rows :], inbc[row_count - rim_rows :]), "ctx", 1
        )
        conv_out = causal_conv(inputs, tail_input, conv_input)
        bc_out = causal_conv(inbc, tail_bc, conv_bc)
        b_part = bc_out[:, 0].reshape(row_count, groups_here, STATE)
        c_part = bc_out[:, 1].reshape(row_count, groups_here, STATE)
        steps_dt = jax.nn.softplus(raw_steps).reshape(row_count, groups_here, per_group)
        decay_rate = -jnp.exp(decay_log).reshape(groups_here, per_group)
        cumul = jnp.cumsum(steps_dt * decay_rate, axis=0)
        order = jnp.arange(row_count, dtype=jnp.int32)
        lower_mask = (order[:, None] >= order[None, :])[:, :, None, None]
        decay_mat = jnp.exp(jnp.where(lower_mask, cumul[:, None] - cumul[None, :], -1e30))
        scores_cb = jnp.einsum("tgn,sgn->gts", c_part, b_part, preferred_element_type=jnp.float32)
        weights = (
            scores_cb[:, None]
            * jnp.transpose(decay_mat, (2, 3, 0, 1))
            * jnp.transpose(steps_dt, (1, 2, 0))[:, :, None, :]
        )
        weights = weights.astype(jnp.bfloat16)
        signal = conv_out.reshape(row_count, groups_here, per_group, head_dim)
        inner_part = jnp.einsum(
            "gkts,sgkp->tgkp", weights, signal, preferred_element_type=jnp.float32
        )
        tail_decay = jnp.exp(cumul[-1][None] - cumul) * steps_dt
        weighted = (signal.astype(jnp.float32) * tail_decay[..., None]).astype(jnp.bfloat16)
        local_state = jnp.einsum(
            "sgkp,sgn->gkpn", weighted, b_part, preferred_element_type=jnp.float32
        )
        block_decay = jnp.exp(cumul[-1])
        count = lax.axis_size("ctx")
        slab = head_dim // count
        pieces = local_state.reshape(heads_here, count, slab, STATE)
        pieces = lax.all_to_all(pieces, "ctx", split_axis=1, concat_axis=0, tiled=False)
        decays = lax.all_gather(block_decay.reshape(heads_here), "ctx")
        held = jnp.zeros(pieces.shape[1:], jnp.float32)
        before = []
        for step in range(count):
            before.append(held)
            held = decays[step][:, None, None] * held + pieces[step]
        incoming = lax.all_to_all(jnp.stack(before), "ctx", split_axis=0, concat_axis=1, tiled=False)
        incoming = incoming.reshape(groups_here, per_group, head_dim, STATE)
        carried = jnp.exp(cumul)[..., None] * jnp.einsum(
            "tgn,gkpn->tgkp", c_part.astype(jnp.float32), incoming, precision=lax.Precision.HIGHEST
        )
        skip_view = skip_gain.reshape(groups_here, per_group)[None, :, :, None]
        mixed_out = inner_part + carried + skip_view * signal.astype(jnp.float32)
        gated = mixed_out.reshape(row_count, feature_width) * jax.nn.silu(gates.astype(jnp.float32))
        square_sum = lax.psum(jnp.sum(gated * gated, axis=1), "tp")
        norm_scale = lax.rsqrt(square_sum / (feature_width * lax.axis_size("tp")) + 1e-05)
        return (gated * norm_scale[:, None] * norm_gain).astype(jnp.bfloat16)

    def attend(queries, micro_kv):
        batch_count = queries.shape[0]
        query_view = queries.reshape(batch_count, row_count, kv_here, per_kv, head_dim)
        query_pos = position + jnp.arange(row_count, dtype=jnp.int32)
        start_max = jnp.full((batch_count, kv_here, per_kv, row_count), -1e30, jnp.float32)
        start_total = jnp.zeros((batch_count, kv_here, per_kv, row_count), jnp.float32)
        start_accum = jnp.zeros((batch_count, kv_here, per_kv, row_count, head_dim), jnp.float32)
        carry = (start_max, start_total, start_accum)
        piece = lax.all_gather(micro_kv, "ctx", axis=1, tiled=True)
        length = piece.shape[1]
        block_rows = math.gcd(length, 512)
        block_count = length // block_rows
        stacked = jnp.moveaxis(
            piece.reshape(batch_count, block_count, block_rows, 2, kv_here, head_dim), 1, 0
        )

        def one_block(held, item):
            block_index, key_block = item
            first_key = block_index * block_rows
            old_max, old_total, old_accum = held
            keys = key_block[:, :, 0]
            values = key_block[:, :, 1]
            logits = (
                jnp.einsum(
                    "btgkp,bsgp->bgkts", query_view, keys, preferred_element_type=jnp.float32
                )
                * factor
            )
            key_pos = first_key + jnp.arange(block_rows, dtype=jnp.int32)
            valid = key_pos[None, :] <= query_pos[:, None]
            masked = jnp.where(valid, logits, -1e30)
            new_max = jnp.maximum(old_max, jnp.max(masked, axis=-1))
            probs = jnp.where(valid, jnp.exp(logits - new_max[..., None]), 0.0)
            rescale = jnp.exp(old_max - new_max)
            new_total = old_total * rescale + jnp.sum(probs, axis=-1)
            product = jnp.einsum(
                "bgkts,bsgp->bgktp",
                probs.astype(jnp.bfloat16),
                values,
                preferred_element_type=jnp.float32,
            )
            new_accum = old_accum * rescale[..., None] + product
            held = (new_max, new_total, new_accum)
            return (held, None)

        carry, _ = lax.scan(one_block, carry, (jnp.arange(block_count, dtype=jnp.int32), stacked))
        final_max, final_total, final_accum = carry
        result = final_accum / final_total[..., None]
        return (
            jnp.transpose(result, (0, 3, 1, 2, 4))
            .reshape(batch_count, row_count, feature_width)
            .astype(jnp.bfloat16)
        )

    own = lax.axis_index("pipe")
    queries = mamba_layer(own)
    return attend(queries[None], lax.dynamic_slice_in_dim(keys_values, own, 1, 0))


def solution(mesh):
    in_specs = (
        P(None, "ctx", "tp"),
        P(None, "ctx", "tp"),
        P(None, "ctx", None, "tp"),
        P(None, "ctx", "tp"),
        P("tp"),
        P("tp"),
        P(None, "tp"),
        P(None, None, "tp"),
        P("tp"),
        P(None, "ctx", None, "tp"),
    )
    out_specs = P("pipe", "ctx", "tp")
    return jax.shard_map(local, mesh=mesh, in_specs=in_specs, out_specs=out_specs, check_vma=False)
```
